32 devices in a mesh: layer: 4 (over x, core), feat: 8 (over z, y).
Axes of the slice: x: 2, y: 2, z: 4, core: 2. Of those that a mesh axis runs over, the one named last changes fastest.
Arguments:
- gradient: bfloat16 [4, 2560, 2560], P('layer', 'feat'), may hold values from -3 to 3
- in_inverse: bfloat16 [4, 2560, 2560], P('layer', 'feat'), may hold values from -1 to 2.5, as said below
- in_coupling: bfloat16 [4, 2560, 2560], P('layer', 'feat'), may hold values from -0.125 to 0.125
- in_carry: bfloat16 [4, 2560, 2560], P('layer', 'feat'), may hold values from -0.125 to 0.125
- out_inverse: bfloat16 [4, 20, 128, 128], P('layer'), may hold values from -1 to 2.5, as said below
- out_coupling: bfloat16 [4, 20, 128, 128], P('layer'), may hold values from -0.5 to 0.5
Outputs:
- update: bfloat16 [4, 2560, 2560], P('layer', 'feat')
The draws below stay inside these ranges and needn't reach their ends.
Inputs may be any that keep to these rules, and one draw needn't show every extreme that they name: `in_inverse`: symmetric in its last two dimensions. `out_inverse`: symmetric in its last two dimensions.
All inputs are finite; a program needn't handle non-finite values.
Results may differ from the reference program's by a relative error of at most 0.006.
Values may be sent and summed in bfloat16 or wider, within the bound.
A program may use at most 64 MiB of HBM per device.

```python
import math
import jax
import jax.numpy as jnp
from jax import lax

DIN = 2560
DOUT = 2560
BLK = 128
LAYERS = 4
OBLOCKS = 20


def symmetric_blocks(key, leading, matrix_order, spread, lower_end, upper_end):
    first_key, second_key = jax.random.split(key)
    noise_part = jax.random.truncated_normal(first_key, -4.0, 4.0, leading + (matrix_order, matrix_order), jnp.float32)
    off_part = (noise_part + jnp.swapaxes(noise_part, -1, -2)) * (spread / math.sqrt(2.0 * matrix_order))
    diagonal = jax.random.uniform(second_key, leading + (matrix_order,), jnp.float32, lower_end, upper_end)
    identity = jnp.eye(matrix_order, dtype=jnp.float32)
    return off_part * (1.0 - identity) + diagonal[..., None] * identity


def draw_in_inverse(key, part):
    matrix = symmetric_blocks(jax.random.fold_in(key, 11), (LAYERS,), DIN, 0.45, 1.0, 2.0)
    return matrix.astype(jnp.bfloat16)


def draw_out_inverse(key, part):
    matrix = symmetric_blocks(jax.random.fold_in(key, 23), (LAYERS, DOUT // BLK), BLK, 0.45, 1.0, 2.0)
    return matrix.astype(jnp.bfloat16)


def level_of(rng, dims, cuts, smallest, top_value):
    loudness, own = 1.0, jax.random.fold_in(rng, 6)
    for axis_at, shards_of in cuts:
        draws = jnp.exp(jax.random.uniform(jax.random.fold_in(own, axis_at), (shards_of,), jnp.float32, smallest / len(cuts), top_value / len(cuts)))
        loudness = loudness * jnp.repeat(draws, dims[axis_at] // shards_of).reshape([-1 if axis == axis_at else 1 for axis in range(len(dims))])
    return loudness


def noise(key, dims, width, limit, shards=(), kind=jnp.bfloat16):
    loudness = level_of(key, dims, shards, -0.22, 0.18) if shards else 1.0
    entries = jax.random.normal(key, dims, jnp.float32) * width * loudness
    return jnp.minimum(jnp.maximum(entries, -limit), limit).astype(kind)


def setup_inputs(seed: int = 0) -> dict:
    key_list = jax.random.split(jax.random.key(seed), 7)
    gradient = noise(key_list[0], (LAYERS, DIN, DOUT), 0.5, 3.0, ((0, 4), (1, 8)))
    in_inverse = draw_in_inverse(jax.random.fold_in(key_list[6], 71), 0)
    in_coupling = noise(key_list[2], (LAYERS, DIN, DIN), DIN ** -0.5, 0.125, ((0, 4), (1, 8)))
    in_carry = noise(key_list[3], (LAYERS, DIN, DIN), DIN ** -0.5, 0.125, ((0, 4), (1, 8)))
    out_inverse = draw_out_inverse(jax.random.fold_in(key_list[6], 71), 0)
    out_coupling = noise(key_list[5], (LAYERS, OBLOCKS, BLK, BLK), BLK ** -0.5, 0.5, ((0, 4),))
    return {"gradient": gradient, "in_inverse": in_inverse, "in_coupling": in_coupling, "in_carry": in_carry, "out_inverse": out_inverse, "out_coupling": out_coupling}


def block_apply(matrix, table, flipped):
    row_count = matrix.shape[0]
    blocks = table.shape[0]
    block_width = table.shape[1]
    grouped = matrix.astype(jnp.float32).reshape(row_count, blocks, block_width)
    pattern = "rnb,ncb->rnc" if flipped else "rnb,nbc->rnc"
    product = jnp.einsum(pattern, grouped, table.astype(jnp.float32), precision=lax.Precision.HIGHEST)
    return product.reshape(row_count, blocks * block_width)


def reference(gradient, in_inverse, in_coupling, in_carry, out_inverse, out_coupling):
    results = []
    pushed_prev = jnp.zeros((DIN, DOUT), jnp.float32)
    for position in range(LAYERS):
        if position + 1 < LAYERS:
            near_rows = block_apply(gradient[position + 1], out_coupling[position], True).astype(jnp.bfloat16)
            coupled = jnp.dot(in_coupling[position], near_rows, preferred_element_type=jnp.float32)
        else:
            coupled = jnp.zeros((DIN, DOUT), jnp.float32)
        reduced = (gradient[position].astype(jnp.float32) - coupled).astype(jnp.bfloat16)
        whitened = jnp.dot(in_inverse[position], reduced, preferred_element_type=jnp.float32).astype(jnp.bfloat16)
        carried = jnp.dot(in_carry[position], reduced, preferred_element_type=jnp.float32).astype(jnp.bfloat16)
        local_term = block_apply(whitened, out_inverse[position], False)
        middle = block_apply(carried, out_inverse[position], False).astype(jnp.bfloat16)
        results.append((local_term - pushed_prev).astype(jnp.bfloat16))
        pushed_prev = block_apply(middle, out_coupling[position], False)
    return jnp.stack(results)
```

```python
import functools

import jax
import jax.numpy as jnp
from jax import lax
from jax.experimental import pallas as pl
from jax.experimental.pallas import tpu as pltpu
from jax.sharding import PartitionSpec as P

MESH = pl.DeviceIdType.MESH
BF = jnp.bfloat16
F32 = jnp.float32
LENT = 7
HOLD = 3


def kernel(nl, nb, nch, lent, g_ref, s_ref, c_ref, k_ref, oi_ref, ps_ref, out_ref,
           w, gl, gn, tab, n_all, r_all, l_st, p_st, l_in, p_in, w2, gl2,
           w_recv, w_send, w_fwd, gl_recv, gl_send, gn_recv, gn_send, t_recv, t_send,
           n_recv, n_send, r_recv, r_send, l_recv, l_send, p_recv, p_send,
           w2_recv, w2_send, w2_fwd, w2_got, gl2_recv, gl2_send):
    r, d = out_ref.shape
    h = d // 2
    cw = h // nch
    blk = ps_ref.shape[1]
    hb = ps_ref.shape[0] // 2
    per = cw // blk
    l = lax.axis_index("layer")
    f = lax.axis_index("feat")
    a, c = l // 2, l % 2
    b, p = f // 2, f % 2
    role = 2 * a + p
    home = c == p
    away = c != p
    chained = role < nl - 1
    core_mate = (2 * a + 1 - c, f)
    swap_mate = (l, 2 * b + 1 - p)
    n_lag = nb - 1
    r_lag = 2 * (nb - 1)
    ahead = min(4, nch)
    first_lent = nch - lent
    halves = w2_send.shape[0]
    piece = r // halves

    def remote(src, dst, ss, rs, dev):
        return pltpu.make_async_remote_copy(
            src_ref=src, dst_ref=dst, send_sem=ss, recv_sem=rs,
            device_id=dev, device_id_type=MESH)

    def arrived(dst, sem):
        pltpu.make_async_copy(dst, dst, sem).wait()

    barrier = pltpu.get_barrier_semaphore()
    for dl in range(1, nl):
        for q in range(2):
            pl.semaphore_signal(barrier, inc=1, device_id=(lax.rem(l + dl, nl), 2 * b + q), device_id_type=MESH)
    pl.semaphore_signal(barrier, inc=1, device_id=swap_mate, device_id_type=MESH)

    @pl.when(b > 0)
    def _():
        pl.semaphore_signal(barrier, inc=1, device_id=(l, f - 2), device_id_type=MESH)

    @pl.when(b < nb - 1)
    def _():
        pl.semaphore_signal(barrier, inc=1, device_id=(l, f + 2), device_id_type=MESH)

    pl.semaphore_wait(barrier, 2 * nl - 1 + jnp.where(b > 0, 1, 0) + jnp.where(b < nb - 1, 1, 0))

    is_end = (b == 0) | (b == nb - 1)
    helps = (b == 1) | (b == nb - 2)
    if not lent:
        is_end = helps = b < 0
    mate_b = jnp.where(b < 2, 1 - b, 2 * nb - 3 - b)
    mate = (l, 2 * mate_b + p)

    def is_lent(k):
        return chained & (k >= first_lent)

    low = l + nl - 1
    low_a, low_p = (low - nl) // 2, lax.rem(low, 2)

    def own_cols(hh, k):
        return g_ref.at[:, pl.ds(pl.multiple_of(hh * h + k * cw, cw), cw)]

    def above_stays(hh):
        return (l >= 1) & (c == 1) & (p == 0) & (c == hh)

    def above_copy(hh, k):
        return remote(own_cols(hh, k), gn.at[k, p], gn_send.at[k, hh], gn_recv.at[k, p],
                      (2 * low_a + hh, 2 * b + low_p))

    def send_above(k, carry):
        for hh in range(2):
            @pl.when(above_stays(hh))
            def _():
                pltpu.make_async_copy(own_cols(hh, k), gn.at[k, p], gn_recv.at[k, p]).start()

            @pl.when((l >= 1) & jnp.logical_not(above_stays(hh)))
            def _():
                above_copy(hh, k).start()
        return carry

    def own_to(hh, k, i, dev):
        return remote(own_cols(hh, k), gl.at[k, p], gl_send.at[k, i], gl_recv.at[k, p], dev)

    def send_own(k, carry):
        @pl.when(home)
        def _():
            pltpu.make_async_copy(own_cols(c, k), gl.at[k, p], gl_recv.at[k, p]).start()
            own_to(1 - c, k, 0, core_mate).start()

        @pl.when(away)
        def _():
            own_to(c, k, 0, swap_mate).start()
            own_to(1 - c, k, 1, (2 * a + 1 - c, 2 * b + 1 - p)).start()
        return carry

    weights = (c_ref, s_ref, k_ref)

    def used(m, layer):
        return (layer < nl - 1) | (m == 1)

    def send_weight(m):
        @pl.when(home & used(m, l))
        def _():
            pltpu.make_async_copy(weights[m], w.at[m, p], w_recv.at[m, p]).start()
            remote(weights[m], w.at[m, p], w_send.at[m], w_recv.at[m, p], core_mate).start()

        @pl.when(away & used(m, l))
        def _():
            remote(weights[m], w.at[m, p], w_send.at[m], w_recv.at[m, p], swap_mate).start()

    lax.fori_loop(0, ahead, send_above, 0)

    @pl.when(home)
    def _():
        pltpu.make_async_copy(ps_ref.at[pl.ds(c * hb, hb)], tab.at[0], t_recv.at[0]).start()
        pltpu.make_async_copy(oi_ref.at[pl.ds(c * hb, hb)], tab.at[1], t_recv.at[1]).start()
        remote(ps_ref.at[pl.ds((1 - c) * hb, hb)], tab.at[0], t_send.at[0], t_recv.at[0], core_mate).start()
        remote(oi_ref.at[pl.ds((1 - c) * hb, hb)], tab.at[1], t_send.at[1], t_recv.at[1], core_mate).start()

    lax.fori_loop(0, ahead, send_own, 0)
    send_weight(0)
    lax.fori_loop(ahead, nch, send_own, 0)
    send_weight(1)
    send_weight(2)

    def take_weight(m, early):
        @pl.when(used(m, role))
        def _():
            arrived(w.at[m, 1 - p], w_recv.at[m, 1 - p])

            @pl.when(home)
            def _():
                remote(w.at[m, 1 - p], w.at[m, 1 - p], w_fwd.at[m], w_recv.at[m, 1 - p], core_mate).start()

            @pl.when((not early) | away)
            def _():
                arrived(w.at[m, p], w_recv.at[m, p])

    def hop(buf, k, src, up, send, recv):
        dev = (l, f + 2) if up else (l, f - 2)
        return remote(buf.at[k, src], buf.at[k, src], send.at[k, src, 0 if up else 1], recv.at[k, src], dev)

    def n_up(k):
        return (b < nb - 1) & jnp.logical_not(is_lent(k) & (b + 1 == nb - 1))

    def n_down(k):
        return (b > 0) & jnp.logical_not(is_lent(k) & (b - 1 == 0))

    def inside(k):
        return (k >= 0) & (k < nch)

    def pass_near(k, j):
        ok = chained & inside(k)
        if j == 0:
            @pl.when(ok & n_up(k))
            def _():
                hop(n_all, k, b, True, n_send, n_recv).start()

            @pl.when(ok & n_down(k))
            def _():
                hop(n_all, k, b, False, n_send, n_recv).start()
        else:
            takes = ok & jnp.logical_not(is_lent(k) & is_end)
            for src, there, onward, up in ((b - j, b - j >= 0, n_up(k), True),
                                           (b + j, b + j < nb, n_down(k), False)):
                @pl.when(takes & there)
                def _():
                    arrived(n_all.at[k, src], n_recv.at[k, src])

                @pl.when(takes & there & onward)
                def _():
                    hop(n_all, k, src, up, n_send, n_recv).start()

    def pass_reduced(k, j):
        ok = inside(k)
        if j == 0:
            makes = ok & jnp.logical_not(is_lent(k) & is_end)

            @pl.when(makes & (b < nb - 1))
            def _():
                hop(r_all, k, b, True, r_send, r_recv).start()

            @pl.when(makes & (b > 0))
            def _():
                hop(r_all, k, b, False, r_send, r_recv).start()
        else:
            if j == 1:
                @pl.when(ok & is_lent(k) & is_end)
                def _():
                    arrived(r_all.at[k, b], r_recv.at[k, b])
            for src, there, onward, up in ((b - j, b - j >= 0, b < nb - 1, True),
                                           (b + j, b + j < nb, b > 0, False)):
                comes = ok & there & jnp.logical_not(is_lent(k) & helps & (src == mate_b))

                @pl.when(comes)
                def _():
                    arrived(r_all.at[k, src], r_recv.at[k, src])

                @pl.when(comes & onward)
                def _():
                    hop(r_all, k, src, up, r_send, r_recv).start()

    for i in range(2):
        arrived(tab.at[i], t_recv.at[i])

    def near_step(k):
        for q in range(2):
            arrived(gn.at[k, q], gn_recv.at[k, q])
        x = gn[k].reshape(2 * r, cw)
        parts = [lax.dot_general(x[:, i * blk:(i + 1) * blk], tab[0, k * per + i],
                                 (((1,), (1,)), ((), ())), preferred_element_type=F32).astype(BF)
                 for i in range(per)]
        n_all[k, b] = jnp.concatenate(parts, axis=1) if per > 1 else parts[0]

    def lend_own(k):
        return remote(gl.at[k], gl2.at[k - first_lent], gl2_send.at[k - first_lent],
                      gl2_recv.at[k - first_lent], mate)

    def rows(i):
        return pl.ds(i * piece, piece)

    def lend_weight(i):
        return remote(w.at[0, c, rows(i)], w2.at[c, rows(i)], w2_send.at[i], w2_recv.at[i], mate)

    def share_weight(i):
        return remote(w2.at[c, rows(i)], w2.at[c, rows(i)], w2_fwd.at[i], w2_got.at[i], core_mate)

    def take_own(k):
        for q in range(2):
            arrived(gl.at[k, q], gl_recv.at[k, q])

    def reduced_step(k):
        @pl.when(chained)
        def _():
            x = n_all[k].reshape(nb * 2 * r, cw)
            coupled = jnp.dot(w[0].reshape(2 * r, d), x, preferred_element_type=F32)
            r_all[k, b] = (gl[k].reshape(2 * r, cw).astype(F32) - coupled).astype(BF)

        @pl.when(jnp.logical_not(chained))
        def _():
            r_all[k, b] = gl[k].reshape(2 * r, cw)

    def reduced_lent(k):
        i = k - first_lent
        arrived(gl2.at[i], gl2_recv.at[i])
        x = n_all[k].reshape(nb * 2 * r, cw)
        coupled = jnp.dot(w2[...].reshape(2 * r, d), x, preferred_element_type=F32)
        r_all[k, mate_b] = (gl2[i].reshape(2 * r, cw).astype(F32) - coupled).astype(BF)
        for up in (True, False):
            hop(r_all, k, mate_b, up, r_send, r_recv).start()

    def local_copy(k, q):
        return remote(l_st.at[k, q], l_in.at[k, c], l_send.at[k, q], l_recv.at[k, c], (role, 2 * b + q))

    def push_copy(k, q):
        return remote(p_st.at[k, q], p_in.at[k, c], p_send.at[k, q], p_recv.at[k, c],
                      (lax.rem(role + 1, nl), 2 * b + q))

    def stays(q, layer):
        return (l == layer) & (p == q)

    def final_step(k, carry):
        x = r_all[k].reshape(nb * 2 * r, cw)
        white = jnp.dot(w[1].reshape(2 * r, d), x, preferred_element_type=F32).astype(BF)
        for i in range(per):
            o = jnp.dot(white[:, i * blk:(i + 1) * blk], tab[1, k * per + i], preferred_element_type=F32)
            l_st[k, :, :, i * blk:(i + 1) * blk] = o.astype(BF).reshape(2, r, blk)
        for q in range(2):
            @pl.when(stays(q, role))
            def _():
                pltpu.make_async_copy(l_st.at[k, q], l_in.at[k, c], l_recv.at[k, c]).start()

            @pl.when(jnp.logical_not(stays(q, role)))
            def _():
                local_copy(k, q).start()

        @pl.when(chained)
        def _():
            y = r_all[k].reshape(nb * 2 * r, cw)
            carried = jnp.dot(w[2].reshape(2 * r, d), y, preferred_element_type=F32).astype(BF)
            for i in range(per):
                mid = jnp.dot(carried[:, i * blk:(i + 1) * blk], tab[1, k * per + i],
                              preferred_element_type=F32).astype(BF)
                o = jnp.dot(mid, tab[0, k * per + i], preferred_element_type=F32)
                p_st[k, :, :, i * blk:(i + 1) * blk] = o.astype(BF).reshape(2, r, blk)
            for q in range(2):
                @pl.when(stays(q, role + 1))
                def _():
                    pltpu.make_async_copy(p_st.at[k, q], p_in.at[k, c], p_recv.at[k, c]).start()

                @pl.when(jnp.logical_not(stays(q, role + 1)))
                def _():
                    push_copy(k, q).start()
        return carry

    def out_step(k, carry):
        for hh in range(2):
            arrived(l_in.at[k, hh], l_recv.at[k, hh])
            dst = pl.ds(pl.multiple_of(hh * h + k * cw, cw), cw)

            @pl.when(l > 0)
            def _():
                arrived(p_in.at[k, hh], p_recv.at[k, hh])
                out_ref[:, dst] = (l_in[k, hh].astype(F32) - p_in[k, hh].astype(F32)).astype(BF)

            @pl.when(l == 0)
            def _():
                out_ref[:, dst] = l_in[k, hh]
        return carry

    held = r_lag + min(HOLD, nch // 2)

    def finals(t):
        return jnp.clip(jnp.minimum(t - r_lag + 1, 2 * (t - held + 1)), 0, nch)

    def step(t, carry):
        @pl.when(t + ahead < nch)
        def _():
            send_above(t + ahead, 0)

        @pl.when(chained & inside(t))
        def _():
            near_step(t)
        for j in range(nb):
            pass_near(t - j, j)

        @pl.when((t == 1) & home & used(0, role))
        def _():
            arrived(w.at[0, p], w_recv.at[0, p])
        kr = t - n_lag

        @pl.when(kr == 0)
        def _():
            take_weight(0, True)
        if lent:
            for i in range(halves):
                @pl.when(chained & is_end & (t == jnp.where(home, 1, n_lag) + i))
                def _():
                    lend_weight(i).start()

            @pl.when(is_end & inside(t - 1) & is_lent(t - 1))
            def _():
                take_own(t - 1)
                lend_own(t - 1).start()

            @pl.when(chained & helps & (kr == first_lent))
            def _():
                for i in range(halves):
                    arrived(w2.at[c, rows(i)], w2_recv.at[i])
                    share_weight(i).start()

        @pl.when(inside(kr) & jnp.logical_not(is_lent(kr) & is_end))
        def _():
            take_own(kr)
            reduced_step(kr)
        pass_reduced(kr, 0)
        if lent:
            @pl.when(chained & helps & (kr == first_lent))
            def _():
                for i in range(halves):
                    arrived(w2.at[1 - c, rows(i)], w2_got.at[i])

            @pl.when(helps & inside(kr) & is_lent(kr))
            def _():
                reduced_lent(kr)
        for j in range(1, nb):
            pass_reduced(kr - j, j)

        @pl.when(t == held)
        def _():
            take_weight(1, False)
            take_weight(2, False)
        lax.fori_loop(finals(t - 1), finals(t), final_step, 0)
        lax.fori_loop(finals(t - 2), finals(t - 1), out_step, 0)
        return carry

    lax.fori_loop(0, nch + r_lag + 1, step, 0)

    def drain(k, carry):
        for src in range(nb):
            @pl.when(chained & (src <= b) & n_up(k) & jnp.logical_not(is_lent(k) & is_end & (src != b)))
            def _():
                hop(n_all, k, src, True, n_send, n_recv).wait_send()

            @pl.when(chained & (src >= b) & n_down(k) & jnp.logical_not(is_lent(k) & is_end & (src != b)))
            def _():
                hop(n_all, k, src, False, n_send, n_recv).wait_send()
            kept = is_lent(k) & is_end & (src == b)
            made = is_lent(k) & helps & (src == mate_b)

            @pl.when((b < nb - 1) & (src <= b) & jnp.logical_not(kept) | made)
            def _():
                hop(r_all, k, src, True, r_send, r_recv).wait_send()

            @pl.when((b > 0) & (src >= b) & jnp.logical_not(kept) | made)
            def _():
                hop(r_all, k, src, False, r_send, r_recv).wait_send()
        for q in range(2):
            @pl.when((l >= 1) & jnp.logical_not(above_stays(q)))
            def _():
                above_copy(q, k).wait_send()

            @pl.when(jnp.logical_not(stays(q, role)))
            def _():
                local_copy(k, q).wait_send()

            @pl.when(chained & jnp.logical_not(stays(q, role + 1)))
            def _():
                push_copy(k, q).wait_send()
        own_to(c, k, 0, swap_mate).wait_send()

        @pl.when(away)
        def _():
            own_to(c, k, 1, swap_mate).wait_send()
        if lent:
            @pl.when(is_lent(k) & is_end)
            def _():
                lend_own(k).wait_send()
        return carry

    lax.fori_loop(0, nch, drain, 0)
    if lent:
        for i in range(halves):
            @pl.when(chained & is_end)
            def _():
                lend_weight(i).wait_send()

            @pl.when(chained & helps)
            def _():
                share_weight(i).wait_send()

    @pl.when(home)
    def _():
        for i, src in enumerate((ps_ref, oi_ref)):
            remote(src.at[pl.ds((1 - c) * hb, hb)], tab.at[i], t_send.at[i], t_recv.at[i], core_mate).wait_send()
    for m in range(3):
        @pl.when(home & used(m, role))
        def _():
            remote(w.at[m, 1 - p], w.at[m, 1 - p], w_fwd.at[m], w_recv.at[m, 1 - p], core_mate).wait_send()

        @pl.when(used(m, l))
        def _():
            remote(weights[m], w.at[m, p], w_send.at[m], w_recv.at[m, p], core_mate).wait_send()


def local(nl, nf, gradient, in_inverse, in_coupling, in_carry, out_inverse, out_coupling):
    g = gradient[0]
    r, d = g.shape
    nb = nf // 2
    blocks, blk = out_inverse.shape[1], out_inverse.shape[2]
    h = d // 2
    hb = blocks // 2
    nch = hb
    cw = h // nch
    lent = nch * LENT // 10 if nb >= 4 and nch >= 4 else 0
    keep = max(lent, 1)
    halves = 2 if r % 32 == 0 else 1
    dma = pltpu.SemaphoreType.DMA
    vm = pltpu.VMEM
    anyspec = pl.BlockSpec(memory_space=pl.ANY)
    out = pl.pallas_call(
        functools.partial(kernel, nl, nb, nch, lent),
        out_shape=jax.ShapeDtypeStruct((r, d), BF),
        in_specs=[anyspec] * 6,
        out_specs=pl.BlockSpec(memory_space=pltpu.VMEM),
        scratch_shapes=[
            vm((3, 2, r, d), BF), vm((nch, 2, r, cw), BF), vm((nch, 2, r, cw), BF), vm((2, hb, blk, blk), BF),
            vm((nch, nb, 2 * r, cw), BF), vm((nch, nb, 2 * r, cw), BF),
            vm((nch, 2, r, cw), BF), vm((nch, 2, r, cw), BF), vm((nch, 2, r, cw), BF), vm((nch, 2, r, cw), BF),
            vm((2, r, d), BF), vm((keep, 2, r, cw), BF),
            dma((3, 2)), dma((3,)), dma((3,)), dma((nch, 2)), dma((nch, 2)), dma((nch, 2)), dma((nch, 2)),
            dma((2,)), dma((2,)),
            dma((nch, nb)), dma((nch, nb, 2)), dma((nch, nb)), dma((nch, nb, 2)),
            dma((nch, 2)), dma((nch, 2)), dma((nch, 2)), dma((nch, 2)),
            dma((halves,)), dma((halves,)), dma((halves,)), dma((halves,)), dma((keep,)), dma((keep,)),
        ],
        compiler_params=pltpu.CompilerParams(
            collective_id=0, has_side_effects=True, vmem_limit_bytes=62 * 1024 * 1024),
    )(g, in_inverse[0], in_coupling[0], in_carry[0], out_inverse[0], out_coupling[0])
    return out[None]


def solution(mesh):
    return jax.shard_map(
        functools.partial(local, mesh.shape["layer"], mesh.shape["feat"]),
        mesh=mesh,
        in_specs=(
            P("layer", "feat", None),
            P("layer", "feat", None),
            P("layer", "feat", None),
            P("layer", "feat", None),
            P("layer", None, None, None),
            P("layer", None, None, None),
        ),
        out_specs=P("layer", "feat", None),
        check_vma=False,
    )
```

```python
import functools

import jax
import jax.numpy as jnp
from jax import lax
from jax.experimental import pallas as pl
from jax.experimental.pallas import tpu as pltpu
from jax.sharding import PartitionSpec as P

MESH = pl.DeviceIdType.MESH
BF = jnp.bfloat16
F32 = jnp.float32
LENT = 6
HOLD = 3
AHEAD = 2
DELAY = 0
SHIFT = 2
HOME_RATE = 2
AWAY_RATE = 3
AWAY_WAIT = 4
IDLE_ABOVE = 1
IDLE_WAIT = 6
IDLE_OWN = 4
OWN_EARLY = 0
IDLE_GAP = 2
S_STEP = 4
K_STEP = 6
IDLE_S = 8
IDLE_K = 9


def kernel(nl, nb, nch, lent, g_ref, s_ref, c_ref, k_ref, oi_ref, ps_ref, out_ref,
           w, gl, gn, tab, n_all, r_all, l_st, p_st, l_in, p_in, w2, gl2,
           w_recv, w_send, w_fwd, gl_recv, gl_send, gn_recv, gn_send, t_recv, t_send,
           n_recv, n_send, r_recv, r_send, l_recv, l_send, p_recv, p_send,
           w2_recv, w2_send, w2_fwd, w2_got, gl2_recv, gl2_send):
    r, d = out_ref.shape
    h = d // 2
    cw = h // nch
    blk = ps_ref.shape[1]
    hb = ps_ref.shape[0] // 2
    per = cw // blk
    l = lax.axis_index("layer")
    f = lax.axis_index("feat")
    a, c = l // 2, l % 2
    b, p = f // 2, f % 2
    role = 2 * a + p
    home = c == p
    away = c != p
    chained = role < nl - 1
    core_mate = (2 * a + 1 - c, f)
    swap_mate = (l, 2 * b + 1 - p)
    n_lag = nb - 1
    r_lag = 2 * (nb - 1) + DELAY + SHIFT - 1
    ahead = min(AHEAD, nch)
    first_lent = nch - lent
    parts = w2_send.shape[0]
    piece = r // parts

    def remote(src, dst, ss, rs, dev):
        return pltpu.make_async_remote_copy(
            src_ref=src, dst_ref=dst, send_sem=ss, recv_sem=rs,
            device_id=dev, device_id_type=MESH)

    def arrived(dst, sem):
        pltpu.make_async_copy(dst, dst, sem).wait()

    barrier = pltpu.get_barrier_semaphore()
    for dl in range(1, nl):
        for q in range(2):
            pl.semaphore_signal(barrier, inc=1, device_id=(lax.rem(l + dl, nl), 2 * b + q), device_id_type=MESH)
    pl.semaphore_signal(barrier, inc=1, device_id=swap_mate, device_id_type=MESH)

    @pl.when(b > 0)
    def _():
        pl.semaphore_signal(barrier, inc=1, device_id=(l, f - 2), device_id_type=MESH)

    @pl.when(b < nb - 1)
    def _():
        pl.semaphore_signal(barrier, inc=1, device_id=(l, f + 2), device_id_type=MESH)

    is_end = (b == 0) | (b == nb - 1)
    helps = (b == 1) | (b == nb - 2)
    if not lent:
        is_end = helps = b < 0
    mate_b = jnp.where(b < 2, 1 - b, 2 * nb - 3 - b)

    @pl.when(is_end | helps)
    def _():
        for core, q in ((c, 1 - p), (1 - c, p), (1 - c, 1 - p)):
            pl.semaphore_signal(barrier, inc=1, device_id=(2 * a + core, 2 * mate_b + q), device_id_type=MESH)

    pl.semaphore_wait(barrier, 2 * nl - 1 + jnp.where(b > 0, 1, 0) + jnp.where(b < nb - 1, 1, 0)
                      + jnp.where(is_end | helps, 3, 0))

    def is_lent(k):
        return chained & (k >= first_lent)

    lends = is_end & (l < nl - 1)

    def at(tt, shift):
        late = chained & (tt >= first_lent)
        k = jnp.where(late, tt - shift, tt)
        return jnp.where((k >= nch) | (late & (k < first_lent)), -1, k)

    low = l + nl - 1
    low_a, low_p = (low - nl) // 2, lax.rem(low, 2)

    def own_cols(hh, k):
        return g_ref.at[:, pl.ds(pl.multiple_of(hh * h + k * cw, cw), cw)]

    def above_stays(hh):
        return (l >= 1) & (c == 1) & (p == 0) & (c == hh)

    def above_copy(hh, k):
        return remote(own_cols(hh, k), gn.at[k, p], gn_send.at[k, hh], gn_recv.at[k, p],
                      (2 * low_a + hh, 2 * b + low_p))

    def send_above(k, carry):
        for hh in range(2):
            @pl.when(above_stays(hh))
            def _():
                pltpu.make_async_copy(own_cols(hh, k), gn.at[k, p], gn_recv.at[k, p]).start()

            @pl.when((l >= 1) & jnp.logical_not(above_stays(hh)))
            def _():
                above_copy(hh, k).start()
        return carry

    def own_to(hh, k, i, dev):
        return remote(own_cols(hh, k), gl.at[k, p], gl_send.at[k, i], gl_recv.at[k, p], dev)

    def send_own(k, carry):
        keeps = jnp.logical_not(lends & (k >= first_lent))

        @pl.when(home & keeps)
        def _():
            pltpu.make_async_copy(own_cols(c, k), gl.at[k, p], gl_recv.at[k, p]).start()
            own_to(1 - c, k, 0, core_mate).start()

        @pl.when(away & keeps)
        def _():
            own_to(c, k, 0, swap_mate).start()
            own_to(1 - c, k, 1, (2 * a + 1 - c, 2 * b + 1 - p)).start()
        return carry

    helper_q = jnp.where(home, p, 1 - p)

    def lend_own(k, i):
        core = c if i == 0 else 1 - c
        return remote(own_cols(core, k), gl2.at[k - first_lent, p], gl2_send.at[k - first_lent, i],
                      gl2_recv.at[k - first_lent, p], (2 * a + core, 2 * mate_b + helper_q))

    def rows(i):
        return pl.ds(pl.multiple_of(i * piece, piece), piece)

    def lend_weight(i):
        return remote(c_ref.at[rows(i)], w2.at[p, rows(i)], w2_send.at[i], w2_recv.at[p, i],
                      (l, 2 * mate_b + helper_q))

    def start_lend(i, carry):
        lend_weight(i).start()
        return carry

    weights = (c_ref, s_ref, k_ref)

    def used(m, layer):
        return (layer < nl - 1) | (m == 1)

    def send_weight(m):
        @pl.when(home & used(m, l))
        def _():
            pltpu.make_async_copy(weights[m], w.at[m, p], w_recv.at[m, p]).start()
            remote(weights[m], w.at[m, p], w_send.at[m], w_recv.at[m, p], core_mate).start()

        @pl.when(away & used(m, l))
        def _():
            remote(weights[m], w.at[m, p], w_send.at[m], w_recv.at[m, p], swap_mate).start()

    lax.fori_loop(0, ahead, send_above, 0)

    @pl.when(home)
    def _():
        pltpu.make_async_copy(ps_ref.at[pl.ds(c * hb, hb)], tab.at[0], t_recv.at[0]).start()
        pltpu.make_async_copy(oi_ref.at[pl.ds(c * hb, hb)], tab.at[1], t_recv.at[1]).start()
        remote(ps_ref.at[pl.ds((1 - c) * hb, hb)], tab.at[0], t_send.at[0], t_recv.at[0], core_mate).start()
        remote(oi_ref.at[pl.ds((1 - c) * hb, hb)], tab.at[1], t_send.at[1], t_recv.at[1], core_mate).start()

    send_own(0, 0)
    send_weight(0)

    def take_weight(m):
        @pl.when(used(m, role))
        def _():
            arrived(w.at[m, 1 - p], w_recv.at[m, 1 - p])

            @pl.when(home)
            def _():
                remote(w.at[m, 1 - p], w.at[m, 1 - p], w_fwd.at[m], w_recv.at[m, 1 - p], core_mate).start()

            arrived(w.at[m, p], w_recv.at[m, p])

    def hop(buf, k, src, up, send, recv):
        dev = (l, f + 2) if up else (l, f - 2)
        return remote(buf.at[k, src], buf.at[k, src], send.at[k, src, 0 if up else 1], recv.at[k, src], dev)

    def n_up(k):
        return (b < nb - 1) & jnp.logical_not(is_lent(k) & (b + 1 == nb - 1))

    def n_down(k):
        return (b > 0) & jnp.logical_not(is_lent(k) & (b - 1 == 0))

    def inside(k):
        return (k >= 0) & (k < nch)

    def pass_near(k, j):
        ok = chained & inside(k)
        if j == 0:
            @pl.when(ok & n_up(k))
            def _():
                hop(n_all, k, b, True, n_send, n_recv).start()

            @pl.when(ok & n_down(k))
            def _():
                hop(n_all, k, b, False, n_send, n_recv).start()
        else:
            takes = ok & jnp.logical_not(is_lent(k) & is_end)
            for src, there, onward, up in ((b - j, b - j >= 0, n_up(k), True),
                                           (b + j, b + j < nb, n_down(k), False)):
                @pl.when(takes & there)
                def _():
                    arrived(n_all.at[k, src], n_recv.at[k, src])

                @pl.when(takes & there & onward)
                def _():
                    hop(n_all, k, src, up, n_send, n_recv).start()

    def pass_reduced(k, j):
        ok = inside(k)
        if j == 0:
            makes = ok & jnp.logical_not(is_lent(k) & is_end)

            @pl.when(makes & (b < nb - 1))
            def _():
                hop(r_all, k, b, True, r_send, r_recv).start()

            @pl.when(makes & (b > 0))
            def _():
                hop(r_all, k, b, False, r_send, r_recv).start()
        else:
            if j == 1:
                @pl.when(ok & is_lent(k) & is_end)
                def _():
                    arrived(r_all.at[k, b], r_recv.at[k, b])
            for src, there, onward, up in ((b - j, b - j >= 0, b < nb - 1, True),
                                           (b + j, b + j < nb, b > 0, False)):
                comes = ok & there & jnp.logical_not(is_lent(k) & helps & (src == mate_b))

                @pl.when(comes)
                def _():
                    arrived(r_all.at[k, src], r_recv.at[k, src])

                @pl.when(comes & onward)
                def _():
                    hop(r_all, k, src, up, r_send, r_recv).start()

    for i in range(2):
        arrived(tab.at[i], t_recv.at[i])

    def near_step(k):
        for q in range(2):
            arrived(gn.at[k, q], gn_recv.at[k, q])
        x = gn[k].reshape(2 * r, cw)
        parts = [lax.dot_general(x[:, i * blk:(i + 1) * blk], tab[0, k * per + i],
                                 (((1,), (1,)), ((), ())), preferred_element_type=F32).astype(BF)
                 for i in range(per)]
        n_all[k, b] = jnp.concatenate(parts, axis=1) if per > 1 else parts[0]

    def share_weight(q):
        return remote(w2.at[q], w2.at[q], w2_fwd.at[q], w2_got.at[q], core_mate)

    def take_lent():
        for q in range(2):
            @pl.when(home)
            def _():
                def got(i, carry):
                    arrived(w2.at[q, rows(i)], w2_recv.at[q, i])
                    return carry

                lax.fori_loop(0, parts, got, 0)
                share_weight(q).start()

    def take_own(k):
        for q in range(2):
            arrived(gl.at[k, q], gl_recv.at[k, q])

    def reduced_step(k):
        @pl.when(chained)
        def _():
            x = n_all[k].reshape(nb * 2 * r, cw)
            coupled = jnp.dot(w[0].reshape(2 * r, d), x, preferred_element_type=F32)
            r_all[k, b] = (gl[k].reshape(2 * r, cw).astype(F32) - coupled).astype(BF)

        @pl.when(jnp.logical_not(chained))
        def _():
            r_all[k, b] = gl[k].reshape(2 * r, cw)

    def reduced_lent(k):
        i = k - first_lent
        for q in range(2):
            arrived(gl2.at[i, q], gl2_recv.at[i, q])
        x = n_all[k].reshape(nb * 2 * r, cw)
        coupled = jnp.dot(w2[...].reshape(2 * r, d), x, preferred_element_type=F32)
        r_all[k, mate_b] = (gl2[i].reshape(2 * r, cw).astype(F32) - coupled).astype(BF)
        for up in (True, False):
            hop(r_all, k, mate_b, up, r_send, r_recv).start()

    def local_copy(k, q):
        return remote(l_st.at[k, q], l_in.at[k, c], l_send.at[k, q], l_recv.at[k, c], (role, 2 * b + q))

    def push_copy(k, q):
        return remote(p_st.at[k, q], p_in.at[k, c], p_send.at[k, q], p_recv.at[k, c],
                      (lax.rem(role + 1, nl), 2 * b + q))

    def stays(q, layer):
        return (l == layer) & (p == q)

    def final_step(k, carry):
        x = r_all[k].reshape(nb * 2 * r, cw)
        white = jnp.dot(w[1].reshape(2 * r, d), x, preferred_element_type=F32).astype(BF)
        for i in range(per):
            o = jnp.dot(white[:, i * blk:(i + 1) * blk], tab[1, k * per + i], preferred_element_type=F32)
            l_st[k, :, :, i * blk:(i + 1) * blk] = o.astype(BF).reshape(2, r, blk)
        for q in range(2):
            @pl.when(stays(q, role))
            def _():
                pltpu.make_async_copy(l_st.at[k, q], l_in.at[k, c], l_recv.at[k, c]).start()

            @pl.when(jnp.logical_not(stays(q, role)))
            def _():
                local_copy(k, q).start()

        @pl.when(chained)
        def _():
            y = r_all[k].reshape(nb * 2 * r, cw)
            carried = jnp.dot(w[2].reshape(2 * r, d), y, preferred_element_type=F32).astype(BF)
            for i in range(per):
                mid = jnp.dot(carried[:, i * blk:(i + 1) * blk], tab[1, k * per + i],
                              preferred_element_type=F32).astype(BF)
                o = jnp.dot(mid, tab[0, k * per + i], preferred_element_type=F32)
                p_st[k, :, :, i * blk:(i + 1) * blk] = o.astype(BF).reshape(2, r, blk)
            for q in range(2):
                @pl.when(stays(q, role + 1))
                def _():
                    pltpu.make_async_copy(p_st.at[k, q], p_in.at[k, c], p_recv.at[k, c]).start()

                @pl.when(jnp.logical_not(stays(q, role + 1)))
                def _():
                    push_copy(k, q).start()
        return carry

    def out_step(k, carry):
        for hh in range(2):
            arrived(l_in.at[k, hh], l_recv.at[k, hh])
            dst = pl.ds(pl.multiple_of(hh * h + k * cw, cw), cw)

            @pl.when(l > 0)
            def _():
                arrived(p_in.at[k, hh], p_recv.at[k, hh])
                out_ref[:, dst] = (l_in[k, hh].astype(F32) - p_in[k, hh].astype(F32)).astype(BF)

            @pl.when(l == 0)
            def _():
                out_ref[:, dst] = l_in[k, hh]
        return carry

    held = r_lag + min(HOLD, nch // 2)

    def finals(t):
        return jnp.clip(jnp.minimum(t - r_lag + 1, 2 * (t - held + 1)), 0, nch)

    def step(t, carry):
        more = jnp.where(chained, at(t + ahead, SHIFT), jnp.where(t - IDLE_ABOVE < nch, t - IDLE_ABOVE, -1))

        @pl.when(more >= ahead)
        def _():
            send_above(more, 0)
        kn = at(t, SHIFT)
        ko = jnp.where(chained, t + OWN_EARLY, t - IDLE_GAP)

        @pl.when((ko >= 1) & (ko < nch))
        def _():
            send_own(ko, 0)
        for m, busy, idle in ((1, S_STEP, IDLE_S), (2, K_STEP, IDLE_K)):
            @pl.when(t == jnp.where(chained, busy, idle))
            def _():
                send_weight(m)

        @pl.when(chained & (kn >= 0))
        def _():
            near_step(kn)
        pass_near(kn, 0)
        if lent:
            @pl.when(lends)
            def _():
                def upto(u):
                    return jnp.clip(jnp.where(home, HOME_RATE * u, AWAY_RATE * (u - jnp.where(chained, AWAY_WAIT, IDLE_WAIT))), 0, parts)

                lax.fori_loop(upto(t), upto(t + 1), start_lend, 0)

            kg = jnp.where(chained, kn, t - IDLE_OWN)

            @pl.when(lends & (kg >= first_lent) & (kg < nch))
            def _():
                for i in range(2):
                    lend_own(kg, i).start()
        for j in range(1, nb):
            pass_near(at(t - j, SHIFT), j)

        kr = at(t - n_lag - DELAY, SHIFT - 1)

        @pl.when(t == n_lag + DELAY)
        def _():
            take_weight(0)
        if lent:
            @pl.when(chained & helps & (t == first_lent + n_lag + DELAY + SHIFT - 2))
            def _():
                take_lent()

        @pl.when(inside(kr) & jnp.logical_not(is_lent(kr) & is_end))
        def _():
            take_own(kr)
            reduced_step(kr)
        pass_reduced(kr, 0)
        if lent:
            @pl.when(chained & helps & away & (kr == first_lent))
            def _():
                for q in range(2):
                    arrived(w2.at[q], w2_got.at[q])

            @pl.when(helps & inside(kr) & is_lent(kr))
            def _():
                reduced_lent(kr)
        for j in range(1, nb):
            pass_reduced(at(t - n_lag - DELAY - j, SHIFT - 1), j)

        @pl.when(t == held)
        def _():
            take_weight(1)
            take_weight(2)
        lax.fori_loop(finals(t - 1), finals(t), final_step, 0)
        lax.fori_loop(finals(t - 2), finals(t - 1), out_step, 0)
        return carry

    lax.fori_loop(0, nch + r_lag + 1, step, 0)

    def drain(k, carry):
        for src in range(nb):
            @pl.when(chained & (src <= b) & n_up(k) & jnp.logical_not(is_lent(k) & is_end & (src != b)))
            def _():
                hop(n_all, k, src, True, n_send, n_recv).wait_send()

            @pl.when(chained & (src >= b) & n_down(k) & jnp.logical_not(is_lent(k) & is_end & (src != b)))
            def _():
                hop(n_all, k, src, False, n_send, n_recv).wait_send()
            kept = is_lent(k) & is_end & (src == b)
            made = is_lent(k) & helps & (src == mate_b)

            @pl.when((b < nb - 1) & (src <= b) & jnp.logical_not(kept) | made)
            def _():
                hop(r_all, k, src, True, r_send, r_recv).wait_send()

            @pl.when((b > 0) & (src >= b) & jnp.logical_not(kept) | made)
            def _():
                hop(r_all, k, src, False, r_send, r_recv).wait_send()
        for q in range(2):
            @pl.when((l >= 1) & jnp.logical_not(above_stays(q)))
            def _():
                above_copy(q, k).wait_send()

            @pl.when(jnp.logical_not(stays(q, role)))
            def _():
                local_copy(k, q).wait_send()

            @pl.when(chained & jnp.logical_not(stays(q, role + 1)))
            def _():
                push_copy(k, q).wait_send()
        gives = lends & (k >= first_lent)

        @pl.when(jnp.logical_not(gives))
        def _():
            own_to(c, k, 0, swap_mate).wait_send()

        @pl.when(away & jnp.logical_not(gives))
        def _():
            own_to(c, k, 1, swap_mate).wait_send()
        if lent:
            @pl.when(gives)
            def _():
                for i in range(2):
                    lend_own(k, i).wait_send()
        return carry

    lax.fori_loop(0, nch, drain, 0)
    if lent:
        def lent_out(i, carry):
            lend_weight(i).wait_send()
            return carry

        @pl.when(lends)
        def _():
            lax.fori_loop(0, parts, lent_out, 0)

        @pl.when(chained & helps & home)
        def _():
            for q in range(2):
                share_weight(q).wait_send()

    @pl.when(home)
    def _():
        for i, src in enumerate((ps_ref, oi_ref)):
            remote(src.at[pl.ds((1 - c) * hb, hb)], tab.at[i], t_send.at[i], t_recv.at[i], core_mate).wait_send()
    for m in range(3):
        @pl.when(home & used(m, role))
        def _():
            remote(w.at[m, 1 - p], w.at[m, 1 - p], w_fwd.at[m], w_recv.at[m, 1 - p], core_mate).wait_send()

        @pl.when(used(m, l))
        def _():
            remote(weights[m], w.at[m, p], w_send.at[m], w_recv.at[m, p], core_mate).wait_send()


def local(nl, nf, gradient, in_inverse, in_coupling, in_carry, out_inverse, out_coupling):
    g = gradient[0]
    r, d = g.shape
    nb = nf // 2
    blocks, blk = out_inverse.shape[1], out_inverse.shape[2]
    h = d // 2
    hb = blocks // 2
    nch = hb
    cw = h // nch
    lent = nch * LENT // 10 if nb >= 4 and nch >= 4 else 0
    keep = max(lent, 1)
    parts = r // 32 if r % 32 == 0 else r // 16 if r % 16 == 0 else 1
    dma = pltpu.SemaphoreType.DMA
    vm = pltpu.VMEM
    anyspec = pl.BlockSpec(memory_space=pl.ANY)
    out = pl.pallas_call(
        functools.partial(kernel, nl, nb, nch, lent),
        out_shape=jax.ShapeDtypeStruct((r, d), BF),
        in_specs=[anyspec] * 6,
        out_specs=pl.BlockSpec(memory_space=pltpu.VMEM),
        scratch_shapes=[
            vm((3, 2, r, d), BF), vm((nch, 2, r, cw), BF), vm((nch, 2, r, cw), BF), vm((2, hb, blk, blk), BF),
            vm((nch, nb, 2 * r, cw), BF), vm((nch, nb, 2 * r, cw), BF),
            vm((nch, 2, r, cw), BF), vm((nch, 2, r, cw), BF), vm((nch, 2, r, cw), BF), vm((nch, 2, r, cw), BF),
            vm((2, r, d), BF), vm((keep, 2, r, cw), BF),
            dma((3, 2)), dma((3,)), dma((3,)), dma((nch, 2)), dma((nch, 2)), dma((nch, 2)), dma((nch, 2)),
            dma((2,)), dma((2,)),
            dma((nch, nb)), dma((nch, nb, 2)), dma((nch, nb)), dma((nch, nb, 2)),
            dma((nch, 2)), dma((nch, 2)), dma((nch, 2)), dma((nch, 2)),
            dma((2, parts)), dma((parts,)), dma((2,)), dma((2,)), dma((keep, 2)), dma((keep, 2)),
        ],
        compiler_params=pltpu.CompilerParams(
            collective_id=0, has_side_effects=True, vmem_limit_bytes=62 * 1024 * 1024),
    )(g, in_inverse[0], in_coupling[0], in_carry[0], out_inverse[0], out_coupling[0])
    return out[None]


def solution(mesh):
    return jax.shard_map(
        functools.partial(local, mesh.shape["layer"], mesh.shape["feat"]),
        mesh=mesh,
        in_specs=(
            P("layer", "feat", None),
            P("layer", "feat", None),
            P("layer", "feat", None),
            P("layer", "feat", None),
            P("layer", None, None, None),
            P("layer", None, None, None),
        ),
        out_specs=P("layer", "feat", None),
        check_vma=False,
    )
```

```python
import functools

import jax
import jax.numpy as jnp
from jax import lax
from jax.experimental import pallas as pl
from jax.experimental.pallas import tpu as pltpu
from jax.sharding import PartitionSpec as P

MESH = pl.DeviceIdType.MESH
BF = jnp.bfloat16
F32 = jnp.float32
LENT = 6
HOLD = 3
AHEAD = 2
DELAY = 0
SHIFT = 2
HOME_RATE = 2
AWAY_RATE = 3
AWAY_WAIT = 4
IDLE_ABOVE = 1
IDLE_WAIT = 6
IDLE_OWN = 4
OWN_EARLY = 0
IDLE_GAP = 2
S_STEP = 4
K_STEP = 6
IDLE_S = 8
IDLE_K = 9


def kernel(nl, nb, nch, lent, g_ref, s_ref, c_ref, k_ref, oi_ref, ps_ref, out_ref,
           w, gl, gn, tab, n_all, r_all, l_st, p_st, l_in, p_in, w2, gl2,
           w_recv, w_send, w_fwd, gl_recv, gl_send, gn_recv, gn_send, t_recv, t_send,
           n_recv, n_send, r_recv, r_send, l_recv, l_send, p_recv, p_send,
           w2_recv, w2_send, w2_fwd, w2_got, gl2_recv, gl2_send):
    r, d = out_ref.shape
    h = d // 2
    cw = h // nch
    blk = ps_ref.shape[1]
    hb = ps_ref.shape[0] // 2
    per = cw // blk
    l = lax.axis_index("layer")
    f = lax.axis_index("feat")
    a, c = l // 2, l % 2
    b, p = f // 2, f % 2
    role = 2 * a + p
    home = c == p
    away = c != p
    chained = role < nl - 1
    core_mate = (2 * a + 1 - c, f)
    swap_mate = (l, 2 * b + 1 - p)
    n_lag = nb - 1
    r_lag = 2 * (nb - 1) + DELAY + SHIFT - 1
    ahead = min(AHEAD, nch)
    first_lent = nch - lent
    parts = r // 32 if r % 32 == 0 else r // 16 if r % 16 == 0 else 1
    piece = r // parts

    def remote(src, dst, ss, rs, dev):
        return pltpu.make_async_remote_copy(
            src_ref=src, dst_ref=dst, send_sem=ss, recv_sem=rs,
            device_id=dev, device_id_type=MESH)

    def arrived(dst, sem):
        pltpu.make_async_copy(dst, dst, sem).wait()

    barrier = pltpu.get_barrier_semaphore()
    for dl in range(1, nl):
        for q in range(2):
            pl.semaphore_signal(barrier, inc=1, device_id=(lax.rem(l + dl, nl), 2 * b + q), device_id_type=MESH)
    pl.semaphore_signal(barrier, inc=1, device_id=swap_mate, device_id_type=MESH)

    @pl.when(b > 0)
    def _():
        pl.semaphore_signal(barrier, inc=1, device_id=(l, f - 2), device_id_type=MESH)

    @pl.when(b < nb - 1)
    def _():
        pl.semaphore_signal(barrier, inc=1, device_id=(l, f + 2), device_id_type=MESH)

    is_end = (b == 0) | (b == nb - 1)
    helps = (b == 1) | (b == nb - 2)
    if not lent:
        is_end = helps = b < 0
    mate_b = jnp.where(b < 2, 1 - b, 2 * nb - 3 - b)

    @pl.when(is_end | helps)
    def _():
        for core, q in ((c, 1 - p), (1 - c, p), (1 - c, 1 - p)):
            pl.semaphore_signal(barrier, inc=1, device_id=(2 * a + core, 2 * mate_b + q), device_id_type=MESH)

    pl.semaphore_wait(barrier, 2 * nl - 1 + jnp.where(b > 0, 1, 0) + jnp.where(b < nb - 1, 1, 0)
                      + jnp.where(is_end | helps, 3, 0))

    def is_lent(k):
        return chained & (k >= first_lent)

    lends = is_end & (l < nl - 1)

    def at(tt, shift):
        late = chained & (tt >= first_lent)
        k = jnp.where(late, tt - shift, tt)
        return jnp.where((k >= nch) | (late & (k < first_lent)), -1, k)

    low = l + nl - 1
    low_a, low_p = (low - nl) // 2, lax.rem(low, 2)

    def own_cols(hh, k):
        return g_ref.at[:, pl.ds(pl.multiple_of(hh * h + k * cw, cw), cw)]

    def above_stays(hh):
        return (l >= 1) & (c == 1) & (p == 0) & (c == hh)

    def above_copy(hh, k):
        return remote(own_cols(hh, k), gn.at[k, p], gn_send.at[hh], gn_recv.at[k],
                      (2 * low_a + hh, 2 * b + low_p))

    def send_above(k, carry):
        for hh in range(2):
            @pl.when(above_stays(hh))
            def _():
                pltpu.make_async_copy(own_cols(hh, k), gn.at[k, p], gn_recv.at[k]).start()

            @pl.when((l >= 1) & jnp.logical_not(above_stays(hh)))
            def _():
                above_copy(hh, k).start()
        return carry

    def own_to(hh, k, i, dev):
        return remote(own_cols(hh, k), gl.at[k, p], gl_send.at[i], gl_recv.at[k], dev)

    def send_own(k, carry):
        keeps = jnp.logical_not(lends & (k >= first_lent))

        @pl.when(home & keeps)
        def _():
            pltpu.make_async_copy(own_cols(c, k), gl.at[k, p], gl_recv.at[k]).start()
            own_to(1 - c, k, 0, core_mate).start()

        @pl.when(away & keeps)
        def _():
            own_to(c, k, 0, swap_mate).start()
            own_to(1 - c, k, 1, (2 * a + 1 - c, 2 * b + 1 - p)).start()
        return carry

    helper_q = jnp.where(home, p, 1 - p)

    def lend_own(k, i):
        core = c if i == 0 else 1 - c
        return remote(own_cols(core, k), gl2.at[k - first_lent, p], gl2_send.at[i],
                      gl2_recv.at[k - first_lent], (2 * a + core, 2 * mate_b + helper_q))

    def rows(i):
        return pl.ds(pl.multiple_of(i * piece, piece), piece)

    def lend_weight(i):
        return remote(c_ref.at[rows(i)], w2.at[p, rows(i)], w2_send.at[0], w2_recv.at[p],
                      (l, 2 * mate_b + helper_q))

    def start_lend(i, carry):
        lend_weight(i).start()
        return carry

    weights = (c_ref, s_ref, k_ref)

    def used(m, layer):
        return (layer < nl - 1) | (m == 1)

    def send_weight(m):
        @pl.when(home & used(m, l))
        def _():
            pltpu.make_async_copy(weights[m], w.at[m, p], w_recv.at[m, p]).start()
            remote(weights[m], w.at[m, p], w_send.at[m], w_recv.at[m, p], core_mate).start()

        @pl.when(away & used(m, l))
        def _():
            remote(weights[m], w.at[m, p], w_send.at[m], w_recv.at[m, p], swap_mate).start()

    lax.fori_loop(0, ahead, send_above, 0)

    @pl.when(home)
    def _():
        pltpu.make_async_copy(ps_ref.at[pl.ds(c * hb, hb)], tab.at[0], t_recv.at[0]).start()
        pltpu.make_async_copy(oi_ref.at[pl.ds(c * hb, hb)], tab.at[1], t_recv.at[1]).start()
        remote(ps_ref.at[pl.ds((1 - c) * hb, hb)], tab.at[0], t_send.at[0], t_recv.at[0], core_mate).start()
        remote(oi_ref.at[pl.ds((1 - c) * hb, hb)], tab.at[1], t_send.at[1], t_recv.at[1], core_mate).start()

    send_own(0, 0)
    send_weight(0)

    def take_weight(m):
        @pl.when(used(m, role))
        def _():
            arrived(w.at[m, 1 - p], w_recv.at[m, 1 - p])

            @pl.when(home)
            def _():
                remote(w.at[m, 1 - p], w.at[m, 1 - p], w_fwd.at[m], w_recv.at[m, 1 - p], core_mate).start()

            arrived(w.at[m, p], w_recv.at[m, p])

    def hop(buf, k, src, up, send, recv):
        dev = (l, f + 2) if up else (l, f - 2)
        return remote(buf.at[k, src], buf.at[k, src], send.at[src, 0 if up else 1], recv.at[k, src], dev)

    def n_up(k):
        return (b < nb - 1) & jnp.logical_not(is_lent(k) & (b + 1 == nb - 1))

    def n_down(k):
        return (b > 0) & jnp.logical_not(is_lent(k) & (b - 1 == 0))

    def inside(k):
        return (k >= 0) & (k < nch)

    def pass_near(k, j):
        ok = chained & inside(k)
        if j == 0:
            @pl.when(ok & n_up(k))
            def _():
                hop(n_all, k, b, True, n_send, n_recv).start()

            @pl.when(ok & n_down(k))
            def _():
                hop(n_all, k, b, False, n_send, n_recv).start()
        else:
            takes = ok & jnp.logical_not(is_lent(k) & is_end)
            for src, there, onward, up in ((b - j, b - j >= 0, n_up(k), True),
                                           (b + j, b + j < nb, n_down(k), False)):
                @pl.when(takes & there)
                def _():
                    arrived(n_all.at[k, src], n_recv.at[k, src])

                @pl.when(takes & there & onward)
                def _():
                    hop(n_all, k, src, up, n_send, n_recv).start()

    def pass_reduced(k, j):
        ok = inside(k)
        if j == 0:
            makes = ok & jnp.logical_not(is_lent(k) & is_end)

            @pl.when(makes & (b < nb - 1))
            def _():
                hop(r_all, k, b, True, r_send, r_recv).start()

            @pl.when(makes & (b > 0))
            def _():
                hop(r_all, k, b, False, r_send, r_recv).start()
        else:
            if j == 1:
                @pl.when(ok & is_lent(k) & is_end)
                def _():
                    arrived(r_all.at[k, b], r_recv.at[k, b])
            for src, there, onward, up in ((b - j, b - j >= 0, b < nb - 1, True),
                                           (b + j, b + j < nb, b > 0, False)):
                comes = ok & there & jnp.logical_not(is_lent(k) & helps & (src == mate_b))

                @pl.when(comes)
                def _():
                    arrived(r_all.at[k, src], r_recv.at[k, src])

                @pl.when(comes & onward)
                def _():
                    hop(r_all, k, src, up, r_send, r_recv).start()

    for i in range(2):
        arrived(tab.at[i], t_recv.at[i])

    def near_step(k):
        arrived(gn.at[k], gn_recv.at[k])
        x = gn[k].reshape(2 * r, cw)
        parts = [lax.dot_general(x[:, i * blk:(i + 1) * blk], tab[0, k * per + i],
                                 (((1,), (1,)), ((), ())), preferred_element_type=F32).astype(BF)
                 for i in range(per)]
        n_all[k, b] = jnp.concatenate(parts, axis=1) if per > 1 else parts[0]

    def share_weight(q):
        return remote(w2.at[q], w2.at[q], w2_fwd.at[q], w2_got.at[q], core_mate)

    def take_lent():
        for q in range(2):
            @pl.when(home)
            def _():
                arrived(w2.at[q], w2_recv.at[q])
                share_weight(q).start()

    def take_own(k):
        arrived(gl.at[k], gl_recv.at[k])

    def reduced_step(k):
        @pl.when(chained)
        def _():
            x = n_all[k].reshape(nb * 2 * r, cw)
            coupled = jnp.dot(w[0].reshape(2 * r, d), x, preferred_element_type=F32)
            r_all[k, b] = (gl[k].reshape(2 * r, cw).astype(F32) - coupled).astype(BF)

        @pl.when(jnp.logical_not(chained))
        def _():
            r_all[k, b] = gl[k].reshape(2 * r, cw)

    def reduced_lent(k):
        i = k - first_lent
        arrived(gl2.at[i], gl2_recv.at[i])
        x = n_all[k].reshape(nb * 2 * r, cw)
        coupled = jnp.dot(w2[...].reshape(2 * r, d), x, preferred_element_type=F32)
        r_all[k, mate_b] = (gl2[i].reshape(2 * r, cw).astype(F32) - coupled).astype(BF)
        for up in (True, False):
            hop(r_all, k, mate_b, up, r_send, r_recv).start()

    def local_copy(k, q):
        return remote(l_st.at[k, q], l_in.at[k, c], l_send.at[q], l_recv.at[k], (role, 2 * b + q))

    def push_copy(k, q):
        return remote(p_st.at[k, q], p_in.at[k, c], p_send.at[q], p_recv.at[k],
                      (lax.rem(role + 1, nl), 2 * b + q))

    def stays(q, layer):
        return (l == layer) & (p == q)

    def final_step(k, carry):
        x = r_all[k].reshape(nb * 2 * r, cw)
        white = jnp.dot(w[1].reshape(2 * r, d), x, preferred_element_type=F32).astype(BF)
        for i in range(per):
            o = jnp.dot(white[:, i * blk:(i + 1) * blk], tab[1, k * per + i], preferred_element_type=F32)
            l_st[k, :, :, i * blk:(i + 1) * blk] = o.astype(BF).reshape(2, r, blk)
        for q in range(2):
            @pl.when(stays(q, role))
            def _():
                pltpu.make_async_copy(l_st.at[k, q], l_in.at[k, c], l_recv.at[k]).start()

            @pl.when(jnp.logical_not(stays(q, role)))
            def _():
                local_copy(k, q).start()

        @pl.when(chained)
        def _():
            y = r_all[k].reshape(nb * 2 * r, cw)
            carried = jnp.dot(w[2].reshape(2 * r, d), y, preferred_element_type=F32).astype(BF)
            for i in range(per):
                mid = jnp.dot(carried[:, i * blk:(i + 1) * blk], tab[1, k * per + i],
                              preferred_element_type=F32).astype(BF)
                o = jnp.dot(mid, tab[0, k * per + i], preferred_element_type=F32)
                p_st[k, :, :, i * blk:(i + 1) * blk] = o.astype(BF).reshape(2, r, blk)
            for q in range(2):
                @pl.when(stays(q, role + 1))
                def _():
                    pltpu.make_async_copy(p_st.at[k, q], p_in.at[k, c], p_recv.at[k]).start()

                @pl.when(jnp.logical_not(stays(q, role + 1)))
                def _():
                    push_copy(k, q).start()
        return carry

    def out_step(k, carry):
        arrived(l_in.at[k], l_recv.at[k])

        @pl.when(l > 0)
        def _():
            arrived(p_in.at[k], p_recv.at[k])
        for hh in range(2):
            dst = pl.ds(pl.multiple_of(hh * h + k * cw, cw), cw)

            @pl.when(l > 0)
            def _():
                out_ref[:, dst] = (l_in[k, hh].astype(F32) - p_in[k, hh].astype(F32)).astype(BF)

            @pl.when(l == 0)
            def _():
                out_ref[:, dst] = l_in[k, hh]
        return carry

    held = r_lag + min(HOLD, nch // 2)

    def finals(t):
        return jnp.clip(jnp.minimum(t - r_lag + 1, 2 * (t - held + 1)), 0, nch)

    def step(t, carry):
        more = jnp.where(chained, at(t + ahead, SHIFT), jnp.where(t - IDLE_ABOVE < nch, t - IDLE_ABOVE, -1))

        @pl.when(more >= ahead)
        def _():
            send_above(more, 0)
        kn = at(t, SHIFT)
        ko = jnp.where(chained, t + OWN_EARLY, t - IDLE_GAP)

        @pl.when((ko >= 1) & (ko < nch))
        def _():
            send_own(ko, 0)
        for m, busy, idle in ((1, S_STEP, IDLE_S), (2, K_STEP, IDLE_K)):
            @pl.when(t == jnp.where(chained, busy, idle))
            def _():
                send_weight(m)

        @pl.when(chained & (kn >= 0))
        def _():
            near_step(kn)
        pass_near(kn, 0)
        if lent:
            @pl.when(lends)
            def _():
                def upto(u):
                    return jnp.clip(jnp.where(home, HOME_RATE * u, AWAY_RATE * (u - jnp.where(chained, AWAY_WAIT, IDLE_WAIT))), 0, parts)

                lax.fori_loop(upto(t), upto(t + 1), start_lend, 0)

            kg = jnp.where(chained, kn, t - IDLE_OWN)

            @pl.when(lends & (kg >= first_lent) & (kg < nch))
            def _():
                for i in range(2):
                    lend_own(kg, i).start()
        for j in range(1, nb):
            pass_near(at(t - j, SHIFT), j)

        kr = at(t - n_lag - DELAY, SHIFT - 1)

        @pl.when(t == n_lag + DELAY)
        def _():
            take_weight(0)
        if lent:
            @pl.when(chained & helps & (t == first_lent + n_lag + DELAY + SHIFT - 2))
            def _():
                take_lent()

        @pl.when(inside(kr) & jnp.logical_not(is_lent(kr) & is_end))
        def _():
            take_own(kr)
            reduced_step(kr)
        pass_reduced(kr, 0)
        if lent:
            @pl.when(chained & helps & away & (kr == first_lent))
            def _():
                for q in range(2):
                    arrived(w2.at[q], w2_got.at[q])

            @pl.when(helps & inside(kr) & is_lent(kr))
            def _():
                reduced_lent(kr)
        for j in range(1, nb):
            pass_reduced(at(t - n_lag - DELAY - j, SHIFT - 1), j)

        @pl.when(t == held)
        def _():
            take_weight(1)
            take_weight(2)
        lax.fori_loop(finals(t - 1), finals(t), final_step, 0)
        lax.fori_loop(finals(t - 2), finals(t - 1), out_step, 0)
        return carry

    lax.fori_loop(0, nch + r_lag + 1, step, 0)

    def settle(ok, buf, count, sem):
        if count:
            @pl.when(ok)
            def _():
                arrived(buf.at[pl.ds(0, count)], sem)

    for src in range(nb):
        for i, (on, edge) in enumerate((((src <= b) & (b < nb - 1), b + 1 == nb - 1),
                                        ((src >= b) & (b > 0), b - 1 == 0))):
            short = edge if lent else b < 0
            settle(chained & on & jnp.logical_not(short), n_all.at[:, src], nch, n_send.at[src, i])
            settle(chained & on & short, n_all.at[:, src], first_lent, n_send.at[src, i])
            kept = chained & is_end & (src == b)
            settle(on & jnp.logical_not(kept), r_all.at[:, src], nch, r_send.at[src, i])
            settle(on & kept, r_all.at[:, src], first_lent, r_send.at[src, i])
            made = chained & helps & (src == mate_b) & jnp.logical_not(on)
            settle(made, r_all.at[:, src], lent, r_send.at[src, i])
    for q in range(2):
        settle((l >= 1) & jnp.logical_not(above_stays(q)), gn.at[:, 0], nch, gn_send.at[q])
        settle(jnp.logical_not(stays(q, role)), l_st.at[:, q], nch, l_send.at[q])
        settle(chained & jnp.logical_not(stays(q, role + 1)), p_st.at[:, q], nch, p_send.at[q])
        sends = away if q else home | away
        settle(sends & jnp.logical_not(lends), gl.at[:, 0], nch, gl_send.at[q])
        settle(sends & lends, gl.at[:, 0], first_lent, gl_send.at[q])
        settle(lends, gl2.at[:, 0], lent, gl2_send.at[q])
    if lent:
        @pl.when(lends)
        def _():
            arrived(w2.at[0], w2_send.at[0])

        @pl.when(chained & helps & home)
        def _():
            for q in range(2):
                share_weight(q).wait_send()

    @pl.when(home)
    def _():
        for i, src in enumerate((ps_ref, oi_ref)):
            remote(src.at[pl.ds((1 - c) * hb, hb)], tab.at[i], t_send.at[i], t_recv.at[i], core_mate).wait_send()
    for m in range(3):
        @pl.when(home & used(m, role))
        def _():
            remote(w.at[m, 1 - p], w.at[m, 1 - p], w_fwd.at[m], w_recv.at[m, 1 - p], core_mate).wait_send()

        @pl.when(used(m, l))
        def _():
            remote(weights[m], w.at[m, p], w_send.at[m], w_recv.at[m, p], core_mate).wait_send()


def local(nl, nf, gradient, in_inverse, in_coupling, in_carry, out_inverse, out_coupling):
    g = gradient[0]
    r, d = g.shape
    nb = nf // 2
    blocks, blk = out_inverse.shape[1], out_inverse.shape[2]
    h = d // 2
    hb = blocks // 2
    nch = hb
    cw = h // nch
    lent = nch * LENT // 10 if nb >= 4 and nch >= 4 else 0
    keep = max(lent, 1)
    dma = pltpu.SemaphoreType.DMA
    vm = pltpu.VMEM
    anyspec = pl.BlockSpec(memory_space=pl.ANY)
    out = pl.pallas_call(
        functools.partial(kernel, nl, nb, nch, lent),
        out_shape=pltpu.VMEM((r, d), BF),
        in_specs=[anyspec] * 6,
        out_specs=pl.BlockSpec(memory_space=pltpu.VMEM),
        scratch_shapes=[
            vm((3, 2, r, d), BF), vm((nch, 2, r, cw), BF), vm((nch, 2, r, cw), BF), vm((2, hb, blk, blk), BF),
            vm((nch, nb, 2 * r, cw), BF), vm((nch, nb, 2 * r, cw), BF),
            vm((nch, 2, r, cw), BF), vm((nch, 2, r, cw), BF), vm((nch, 2, r, cw), BF), vm((nch, 2, r, cw), BF),
            vm((2, r, d), BF), vm((keep, 2, r, cw), BF),
            dma((3, 2)), dma((3,)), dma((3,)), dma((nch,)), dma((2,)), dma((nch,)), dma((2,)),
            dma((2,)), dma((2,)),
            dma((nch, nb)), dma((nb, 2)), dma((nch, nb)), dma((nb, 2)),
            dma((nch,)), dma((2,)), dma((nch,)), dma((2,)),
            dma((2,)), dma((1,)), dma((2,)), dma((2,)), dma((keep,)), dma((2,)),
        ],
        compiler_params=pltpu.CompilerParams(
            collective_id=0, has_side_effects=True, vmem_limit_bytes=62 * 1024 * 1024),
    )(g, in_inverse[0], in_coupling[0], in_carry[0], out_inverse[0], out_coupling[0])
    return out[None]


def solution(mesh):
    return jax.shard_map(
        functools.partial(local, mesh.shape["layer"], mesh.shape["feat"]),
        mesh=mesh,
        in_specs=(
            P("layer", "feat", None),
            P("layer", "feat", None),
            P("layer", "feat", None),
            P("layer", "feat", None),
            P("layer", None, None, None),
            P("layer", None, None, None),
        ),
        out_specs=P("layer", "feat", None),
        check_vma=False,
    )
```

```python
import functools

import jax
import jax.numpy as jnp
from jax import lax
from jax.experimental import pallas as pl
from jax.experimental.pallas import tpu as pltpu
from jax.sharding import PartitionSpec as P

MESH = pl.DeviceIdType.MESH
BF = jnp.bfloat16
F32 = jnp.float32
LENT = 6
HOLD = 3
AHEAD = 2
DELAY = 0
SHIFT = 2
HOME_RATE = 2
AWAY_RATE = 4
AWAY_WAIT = 4
IDLE_ABOVE = 2
IDLE_WAIT = 7
IDLE_OWN = 4
OWN_EARLY = 0
IDLE_GAP = 2
S_STEP = 4
K_STEP = 6
IDLE_S = 8
IDLE_K = 9


def kernel(nl, nb, nch, lent, g_ref, s_ref, c_ref, k_ref, oi_ref, ps_ref, out_ref,
           w, gl, gn, tab, n_all, r_all, l_st, p_st, l_in, p_in, w2, gl2,
           w_recv, w_send, w_fwd, gl_recv, gl_send, gn_recv, gn_send, t_recv, t_send,
           n_recv, n_send, r_recv, r_send, l_recv, l_send, p_recv, p_send,
           w2_recv, w2_send, w2_fwd, w2_got, gl2_recv, gl2_send):
    r, d = out_ref.shape
    h = d // 2
    cw = h // nch
    blk = ps_ref.shape[1]
    hb = ps_ref.shape[0] // 2
    per = cw // blk
    l = lax.axis_index("layer")
    f = lax.axis_index("feat")
    a, c = l // 2, l % 2
    b, p = f // 2, f % 2
    role = 2 * a + p
    home = c == p
    away = c != p
    chained = role < nl - 1
    core_mate = (2 * a + 1 - c, f)
    swap_mate = (l, 2 * b + 1 - p)
    n_lag = nb - 1
    r_lag = 2 * (nb - 1) + DELAY + SHIFT - 1
    ahead = min(AHEAD, nch)
    first_lent = nch - lent
    parts = r // 32 if r % 32 == 0 else r // 16 if r % 16 == 0 else 1
    piece = r // parts

    def remote(src, dst, ss, rs, dev):
        return pltpu.make_async_remote_copy(
            src_ref=src, dst_ref=dst, send_sem=ss, recv_sem=rs,
            device_id=dev, device_id_type=MESH)

    def arrived(dst, sem):
        pltpu.make_async_copy(dst, dst, sem).wait()

    barrier = pltpu.get_barrier_semaphore()
    for dl in range(1, nl):
        for q in range(2):
            pl.semaphore_signal(barrier, inc=1, device_id=(lax.rem(l + dl, nl), 2 * b + q), device_id_type=MESH)
    pl.semaphore_signal(barrier, inc=1, device_id=swap_mate, device_id_type=MESH)

    @pl.when(b > 0)
    def _():
        pl.semaphore_signal(barrier, inc=1, device_id=(l, f - 2), device_id_type=MESH)

    @pl.when(b < nb - 1)
    def _():
        pl.semaphore_signal(barrier, inc=1, device_id=(l, f + 2), device_id_type=MESH)

    is_end = (b == 0) | (b == nb - 1)
    helps = (b == 1) | (b == nb - 2)
    if not lent:
        is_end = helps = b < 0
    mate_b = jnp.where(b < 2, 1 - b, 2 * nb - 3 - b)

    @pl.when(is_end | helps)
    def _():
        for core, q in ((c, 1 - p), (1 - c, p), (1 - c, 1 - p)):
            pl.semaphore_signal(barrier, inc=1, device_id=(2 * a + core, 2 * mate_b + q), device_id_type=MESH)

    pl.semaphore_wait(barrier, 2 * nl - 1 + jnp.where(b > 0, 1, 0) + jnp.where(b < nb - 1, 1, 0)
                      + jnp.where(is_end | helps, 3, 0))

    def is_lent(k):
        return chained & (k >= first_lent)

    lends = is_end & (l < nl - 1)

    def at(tt, shift):
        late = chained & (tt >= first_lent)
        k = jnp.where(late, tt - shift, tt)
        return jnp.where((k >= nch) | (late & (k < first_lent)), -1, k)

    low = l + nl - 1
    low_a, low_p = (low - nl) // 2, lax.rem(low, 2)

    def own_cols(hh, k):
        return g_ref.at[:, pl.ds(pl.multiple_of(hh * h + k * cw, cw), cw)]

    def above_stays(hh):
        return (l >= 1) & (c == 1) & (p == 0) & (c == hh)

    def above_copy(hh, k):
        return remote(own_cols(hh, k), gn.at[k, p], gn_send.at[hh], gn_recv.at[k],
                      (2 * low_a + hh, 2 * b + low_p))

    def send_above(k, carry):
        for hh in range(2):
            @pl.when(above_stays(hh))
            def _():
                pltpu.make_async_copy(own_cols(hh, k), gn.at[k, p], gn_recv.at[k]).start()

            @pl.when((l >= 1) & jnp.logical_not(above_stays(hh)))
            def _():
                above_copy(hh, k).start()
        return carry

    def own_to(hh, k, i, dev):
        return remote(own_cols(hh, k), gl.at[k, p], gl_send.at[i], gl_recv.at[k], dev)

    def send_own(k, carry):
        keeps = jnp.logical_not(lends & (k >= first_lent))

        @pl.when(home & keeps)
        def _():
            pltpu.make_async_copy(own_cols(c, k), gl.at[k, p], gl_recv.at[k]).start()
            own_to(1 - c, k, 0, core_mate).start()

        @pl.when(away & keeps)
        def _():
            own_to(c, k, 0, swap_mate).start()
            own_to(1 - c, k, 1, (2 * a + 1 - c, 2 * b + 1 - p)).start()
        return carry

    helper_q = jnp.where(home, p, 1 - p)

    def lend_own(k, i):
        core = c if i == 0 else 1 - c
        return remote(own_cols(core, k), gl2.at[k - first_lent, p], gl2_send.at[i],
                      gl2_recv.at[k - first_lent], (2 * a + core, 2 * mate_b + helper_q))

    def rows(i):
        return pl.ds(pl.multiple_of(i * piece, piece), piece)

    def lend_weight(i):
        return remote(c_ref.at[rows(i)], w2.at[p, rows(i)], w2_send.at[0], w2_recv.at[p],
                      (l, 2 * mate_b + helper_q))

    def start_lend(i, carry):
        lend_weight(i).start()
        return carry

    weights = (c_ref, s_ref, k_ref)

    def used(m, layer):
        return (layer < nl - 1) | (m == 1)

    def send_weight(m):
        @pl.when(home & used(m, l))
        def _():
            pltpu.make_async_copy(weights[m], w.at[m, p], w_recv.at[m, p]).start()
            remote(weights[m], w.at[m, p], w_send.at[m], w_recv.at[m, p], core_mate).start()

        @pl.when(away & used(m, l))
        def _():
            remote(weights[m], w.at[m, p], w_send.at[m], w_recv.at[m, p], swap_mate).start()

    lax.fori_loop(0, ahead, send_above, 0)

    @pl.when(home)
    def _():
        pltpu.make_async_copy(ps_ref.at[pl.ds(c * hb, hb)], tab.at[0], t_recv.at[0]).start()
        pltpu.make_async_copy(oi_ref.at[pl.ds(c * hb, hb)], tab.at[1], t_recv.at[1]).start()
        remote(ps_ref.at[pl.ds((1 - c) * hb, hb)], tab.at[0], t_send.at[0], t_recv.at[0], core_mate).start()
        remote(oi_ref.at[pl.ds((1 - c) * hb, hb)], tab.at[1], t_send.at[1], t_recv.at[1], core_mate).start()

    send_own(0, 0)
    send_weight(0)

    def take_weight(m):
        @pl.when(used(m, role))
        def _():
            arrived(w.at[m, 1 - p], w_recv.at[m, 1 - p])

            @pl.when(home)
            def _():
                remote(w.at[m, 1 - p], w.at[m, 1 - p], w_fwd.at[m], w_recv.at[m, 1 - p], core_mate).start()

            arrived(w.at[m, p], w_recv.at[m, p])

    def hop(buf, k, src, up, send, recv):
        dev = (l, f + 2) if up else (l, f - 2)
        return remote(buf.at[k, src], buf.at[k, src], send.at[src, 0 if up else 1], recv.at[k, src], dev)

    def n_up(k):
        return (b < nb - 1) & jnp.logical_not(is_lent(k) & (b + 1 == nb - 1))

    def n_down(k):
        return (b > 0) & jnp.logical_not(is_lent(k) & (b - 1 == 0))

    def inside(k):
        return (k >= 0) & (k < nch)

    def pass_near(k, j):
        ok = chained & inside(k)
        if j == 0:
            @pl.when(ok & n_up(k))
            def _():
                hop(n_all, k, b, True, n_send, n_recv).start()

            @pl.when(ok & n_down(k))
            def _():
                hop(n_all, k, b, False, n_send, n_recv).start()
        else:
            takes = ok & jnp.logical_not(is_lent(k) & is_end)
            for src, there, onward, up in ((b - j, b - j >= 0, n_up(k), True),
                                           (b + j, b + j < nb, n_down(k), False)):
                @pl.when(takes & there)
                def _():
                    arrived(n_all.at[k, src], n_recv.at[k, src])

                @pl.when(takes & there & onward)
                def _():
                    hop(n_all, k, src, up, n_send, n_recv).start()

    def pass_reduced(k, j):
        ok = inside(k)
        if j == 0:
            makes = ok & jnp.logical_not(is_lent(k) & is_end)

            @pl.when(makes & (b < nb - 1))
            def _():
                hop(r_all, k, b, True, r_send, r_recv).start()

            @pl.when(makes & (b > 0))
            def _():
                hop(r_all, k, b, False, r_send, r_recv).start()
        else:
            if j == 1:
                @pl.when(ok & is_lent(k) & is_end)
                def _():
                    arrived(r_all.at[k, b], r_recv.at[k, b])
            for src, there, onward, up in ((b - j, b - j >= 0, b < nb - 1, True),
                                           (b + j, b + j < nb, b > 0, False)):
                comes = ok & there & jnp.logical_not(is_lent(k) & helps & (src == mate_b))

                @pl.when(comes)
                def _():
                    arrived(r_all.at[k, src], r_recv.at[k, src])

                @pl.when(comes & onward)
                def _():
                    hop(r_all, k, src, up, r_send, r_recv).start()

    for i in range(2):
        arrived(tab.at[i], t_recv.at[i])

    def near_step(k):
        arrived(gn.at[k], gn_recv.at[k])
        x = gn[k].reshape(2 * r, cw)
        parts = [lax.dot_general(x[:, i * blk:(i + 1) * blk], tab[0, k * per + i],
                                 (((1,), (1,)), ((), ())), preferred_element_type=F32).astype(BF)
                 for i in range(per)]
        n_all[k, b] = jnp.concatenate(parts, axis=1) if per > 1 else parts[0]

    def share_weight(q):
        return remote(w2.at[q], w2.at[q], w2_fwd.at[q], w2_got.at[q], core_mate)

    def take_lent():
        for q in range(2):
            @pl.when(home)
            def _():
                arrived(w2.at[q], w2_recv.at[q])
                share_weight(q).start()

    def take_own(k):
        arrived(gl.at[k], gl_recv.at[k])

    def reduced_step(k):
        @pl.when(chained)
        def _():
            x = n_all[k].reshape(nb * 2 * r, cw)
            coupled = jnp.dot(w[0].reshape(2 * r, d), x, preferred_element_type=F32)
            r_all[k, b] = (gl[k].reshape(2 * r, cw).astype(F32) - coupled).astype(BF)

        @pl.when(jnp.logical_not(chained))
        def _():
            r_all[k, b] = gl[k].reshape(2 * r, cw)

    def reduced_lent(k):
        i = k - first_lent
        arrived(gl2.at[i], gl2_recv.at[i])
        x = n_all[k].reshape(nb * 2 * r, cw)
        coupled = jnp.dot(w2[...].reshape(2 * r, d), x, preferred_element_type=F32)
        r_all[k, mate_b] = (gl2[i].reshape(2 * r, cw).astype(F32) - coupled).astype(BF)
        for up in (True, False):
            hop(r_all, k, mate_b, up, r_send, r_recv).start()

    def local_copy(k, q):
        return remote(l_st.at[k, q], l_in.at[k, c], l_send.at[q], l_recv.at[k], (role, 2 * b + q))

    def push_copy(k, q):
        return remote(p_st.at[k, q], p_in.at[k, c], p_send.at[q], p_recv.at[k],
                      (lax.rem(role + 1, nl), 2 * b + q))

    def stays(q, layer):
        return (l == layer) & (p == q)

    def final_step(k, carry):
        x = r_all[k].reshape(nb * 2 * r, cw)
        white = jnp.dot(w[1].reshape(2 * r, d), x, preferred_element_type=F32).astype(BF)
        for i in range(per):
            o = jnp.dot(white[:, i * blk:(i + 1) * blk], tab[1, k * per + i], preferred_element_type=F32)
            l_st[k, :, :, i * blk:(i + 1) * blk] = o.astype(BF).reshape(2, r, blk)
        for q in range(2):
            @pl.when(stays(q, role))
            def _():
                pltpu.make_async_copy(l_st.at[k, q], l_in.at[k, c], l_recv.at[k]).start()

            @pl.when(jnp.logical_not(stays(q, role)))
            def _():
                local_copy(k, q).start()

        @pl.when(chained)
        def _():
            y = r_all[k].reshape(nb * 2 * r, cw)
            carried = jnp.dot(w[2].reshape(2 * r, d), y, preferred_element_type=F32).astype(BF)
            for i in range(per):
                mid = jnp.dot(carried[:, i * blk:(i + 1) * blk], tab[1, k * per + i],
                              preferred_element_type=F32).astype(BF)
                o = jnp.dot(mid, tab[0, k * per + i], preferred_element_type=F32)
                p_st[k, :, :, i * blk:(i + 1) * blk] = o.astype(BF).reshape(2, r, blk)
            for q in range(2):
                @pl.when(stays(q, role + 1))
                def _():
                    pltpu.make_async_copy(p_st.at[k, q], p_in.at[k, c], p_recv.at[k]).start()

                @pl.when(jnp.logical_not(stays(q, role + 1)))
                def _():
                    push_copy(k, q).start()
        return carry

    def out_step(k, carry):
        arrived(l_in.at[k], l_recv.at[k])

        @pl.when(l > 0)
        def _():
            arrived(p_in.at[k], p_recv.at[k])
        for hh in range(2):
            dst = pl.ds(pl.multiple_of(hh * h + k * cw, cw), cw)

            @pl.when(l > 0)
            def _():
                out_ref[:, dst] = (l_in[k, hh].astype(F32) - p_in[k, hh].astype(F32)).astype(BF)

            @pl.when(l == 0)
            def _():
                out_ref[:, dst] = l_in[k, hh]
        return carry

    held = r_lag + min(HOLD, nch // 2)

    def finals(t):
        return jnp.clip(jnp.minimum(t - r_lag + 1, 2 * (t - held + 1)), 0, nch)

    def step(t, carry):
        more = jnp.where(chained, at(t + ahead, SHIFT), jnp.where(t - IDLE_ABOVE < nch, t - IDLE_ABOVE, -1))

        @pl.when(more >= ahead)
        def _():
            send_above(more, 0)
        kn = at(t, SHIFT)
        ko = jnp.where(chained, t + OWN_EARLY, t - IDLE_GAP)

        @pl.when((ko >= 1) & (ko < nch))
        def _():
            send_own(ko, 0)
        for m, busy, idle in ((1, S_STEP, IDLE_S), (2, K_STEP, IDLE_K)):
            @pl.when(t == jnp.where(chained, busy, idle))
            def _():
                send_weight(m)

        @pl.when(chained & (kn >= 0))
        def _():
            near_step(kn)
        pass_near(kn, 0)
        if lent:
            @pl.when(lends)
            def _():
                def upto(u):
                    return jnp.clip(jnp.where(home, HOME_RATE * u, AWAY_RATE * (u - jnp.where(chained, AWAY_WAIT, IDLE_WAIT))), 0, parts)

                lax.fori_loop(upto(t), upto(t + 1), start_lend, 0)

            kg = jnp.where(chained, kn, t - IDLE_OWN)

            @pl.when(lends & (kg >= first_lent) & (kg < nch))
            def _():
                for i in range(2):
                    lend_own(kg, i).start()
        for j in range(1, nb):
            pass_near(at(t - j, SHIFT), j)

        kr = at(t - n_lag - DELAY, SHIFT - 1)

        @pl.when(t == n_lag + DELAY)
        def _():
            take_weight(0)
        if lent:
            @pl.when(chained & helps & (t == first_lent + n_lag + DELAY + SHIFT - 2))
            def _():
                take_lent()

        @pl.when(inside(kr) & jnp.logical_not(is_lent(kr) & is_end))
        def _():
            take_own(kr)
            reduced_step(kr)
        pass_reduced(kr, 0)
        if lent:
            @pl.when(chained & helps & away & (kr == first_lent))
            def _():
                for q in range(2):
                    arrived(w2.at[q], w2_got.at[q])

            @pl.when(helps & inside(kr) & is_lent(kr))
            def _():
                reduced_lent(kr)
        for j in range(1, nb):
            pass_reduced(at(t - n_lag - DELAY - j, SHIFT - 1), j)

        @pl.when(t == held)
        def _():
            take_weight(1)
            take_weight(2)
        lax.fori_loop(finals(t - 1), finals(t), final_step, 0)
        lax.fori_loop(finals(t - 2), finals(t - 1), out_step, 0)
        return carry

    lax.fori_loop(0, nch + r_lag + 1, step, 0)

    def settle(ok, buf, count, sem):
        if count:
            @pl.when(ok)
            def _():
                arrived(buf.at[pl.ds(0, count)], sem)

    for src in range(nb):
        for i, (on, edge) in enumerate((((src <= b) & (b < nb - 1), b + 1 == nb - 1),
                                        ((src >= b) & (b > 0), b - 1 == 0))):
            short = edge if lent else b < 0
            settle(chained & on & jnp.logical_not(short), n_all.at[:, src], nch, n_send.at[src, i])
            settle(chained & on & short, n_all.at[:, src], first_lent, n_send.at[src, i])
            kept = chained & is_end & (src == b)
            settle(on & jnp.logical_not(kept), r_all.at[:, src], nch, r_send.at[src, i])
            settle(on & kept, r_all.at[:, src], first_lent, r_send.at[src, i])
            made = chained & helps & (src == mate_b) & jnp.logical_not(on)
            settle(made, r_all.at[:, src], lent, r_send.at[src, i])
    for q in range(2):
        settle((l >= 1) & jnp.logical_not(above_stays(q)), gn.at[:, 0], nch, gn_send.at[q])
        settle(jnp.logical_not(stays(q, role)), l_st.at[:, q], nch, l_send.at[q])
        settle(chained & jnp.logical_not(stays(q, role + 1)), p_st.at[:, q], nch, p_send.at[q])
        sends = away if q else home | away
        settle(sends & jnp.logical_not(lends), gl.at[:, 0], nch, gl_send.at[q])
        settle(sends & lends, gl.at[:, 0], first_lent, gl_send.at[q])
        settle(lends, gl2.at[:, 0], lent, gl2_send.at[q])
    if lent:
        @pl.when(lends)
        def _():
            arrived(w2.at[0], w2_send.at[0])

        @pl.when(chained & helps & home)
        def _():
            for q in range(2):
                share_weight(q).wait_send()

    @pl.when(home)
    def _():
        for i, src in enumerate((ps_ref, oi_ref)):
            remote(src.at[pl.ds((1 - c) * hb, hb)], tab.at[i], t_send.at[i], t_recv.at[i], core_mate).wait_send()
    for m in range(3):
        @pl.when(home & used(m, role))
        def _():
            remote(w.at[m, 1 - p], w.at[m, 1 - p], w_fwd.at[m], w_recv.at[m, 1 - p], core_mate).wait_send()

        @pl.when(used(m, l))
        def _():
            remote(weights[m], w.at[m, p], w_send.at[m], w_recv.at[m, p], core_mate).wait_send()


def local(nl, nf, gradient, in_inverse, in_coupling, in_carry, out_inverse, out_coupling):
    g = gradient[0]
    r, d = g.shape
    nb = nf // 2
    blocks, blk = out_inverse.shape[1], out_inverse.shape[2]
    h = d // 2
    hb = blocks // 2
    nch = hb
    cw = h // nch
    lent = nch * LENT // 10 if nb >= 4 and nch >= 4 else 0
    keep = max(lent, 1)
    dma = pltpu.SemaphoreType.DMA
    vm = pltpu.VMEM
    anyspec = pl.BlockSpec(memory_space=pl.ANY)
    out = pl.pallas_call(
        functools.partial(kernel, nl, nb, nch, lent),
        out_shape=pltpu.VMEM((r, d), BF),
        in_specs=[anyspec] * 6,
        out_specs=pl.BlockSpec(memory_space=pltpu.VMEM),
        scratch_shapes=[
            vm((3, 2, r, d), BF), vm((nch, 2, r, cw), BF), vm((nch, 2, r, cw), BF), vm((2, hb, blk, blk), BF),
            vm((nch, nb, 2 * r, cw), BF), vm((nch, nb, 2 * r, cw), BF),
            vm((nch, 2, r, cw), BF), vm((nch, 2, r, cw), BF), vm((nch, 2, r, cw), BF), vm((nch, 2, r, cw), BF),
            vm((2, r, d), BF), vm((keep, 2, r, cw), BF),
            dma((3, 2)), dma((3,)), dma((3,)), dma((nch,)), dma((2,)), dma((nch,)), dma((2,)),
            dma((2,)), dma((2,)),
            dma((nch, nb)), dma((nb, 2)), dma((nch, nb)), dma((nb, 2)),
            dma((nch,)), dma((2,)), dma((nch,)), dma((2,)),
            dma((2,)), dma((1,)), dma((2,)), dma((2,)), dma((keep,)), dma((2,)),
        ],
        compiler_params=pltpu.CompilerParams(
            collective_id=0, has_side_effects=True, vmem_limit_bytes=62 * 1024 * 1024),
    )(g, in_inverse[0], in_coupling[0], in_carry[0], out_inverse[0], out_coupling[0])
    return out[None]


def solution(mesh):
    return jax.shard_map(
        functools.partial(local, mesh.shape["layer"], mesh.shape["feat"]),
        mesh=mesh,
        in_specs=(
            P("layer", "feat", None),
            P("layer", "feat", None),
            P("layer", "feat", None),
            P("layer", "feat", None),
            P("layer", None, None, None),
            P("layer", None, None, None),
        ),
        out_specs=P("layer", "feat", None),
        check_vma=False,
    )
```
